32 devices in a mesh: segment: 4 (over z), ctx: 4 (over y, x), tp: 2 (over core).
Axes of the slice: x: 2, y: 2, z: 4, core: 2. Of those that a mesh axis runs over, the one named last changes fastest.
Arguments:
- queries: bfloat16 [4, 512, 8, 640], P('segment', 'ctx', 'tp'), may hold values from -200 to 200
- pairs: bfloat16 [4, 512, 8, 256], P('segment', 'ctx', 'tp'), may hold values from -6 to 6
- out_proj: bfloat16 [4, 8, 640, 5120], P('segment', 'tp'), may hold values from -0.625 to 0.625
- lengths: int32 [4, 4], replicated, may hold values from 1 to 256, 512 in all within a row
Outputs:
- scored: bfloat16 [4, 512, 5120], P('segment', 'ctx', 'tp')
The draws below stay inside these ranges and needn't reach their ends.
Inputs may be any that keep to these rules, and one draw needn't show every extreme that they name: `lengths`: each row sums to 512; its largest length is exactly 256.
All inputs are finite; a program needn't handle non-finite values.
Results may differ from the reference program's by a relative error of at most 0.014.
Values may be sent and summed in bfloat16 or wider, within the bound.
A program may use at most 64 MiB of HBM per device.

```python
import math
import jax
import jax.numpy as jnp
import numpy as np
from jax import lax

D = 5120
HEADS = 40
KVH = 8
HD = 128
ROLLS = 4
GROUP = 5
SEQ = 512
MBATCH = 4
N_TP = 2


def base_draw(key):
    shape = (MBATCH, SEQ, KVH, HD)
    key_part = jnp.clip(jax.random.normal(jax.random.fold_in(key, 101), shape, jnp.float32), -6.0, 6.0)
    value_part = jnp.clip(jax.random.normal(jax.random.fold_in(key, 102), shape, jnp.float32), -6.0, 6.0)
    query_part = jnp.clip(jax.random.normal(jax.random.fold_in(key, 103), (MBATCH, SEQ, KVH, GROUP, HD), jnp.float32), -6.0, 6.0)
    return (query_part, key_part, value_part)


def draw_queries(key, part):
    query_part, key_part, value_part = base_draw(key)
    return query_part.reshape(MBATCH, SEQ, KVH, GROUP * HD).astype(jnp.bfloat16)


def draw_pairs(key, part):
    query_part, key_part, value_part = base_draw(key)
    return jnp.concatenate([key_part, value_part], axis=3).astype(jnp.bfloat16)


def levels(own_key, extent, pieces, low, high):
    factor_of = 1.0
    for position, shards_of in pieces:
        steps = jax.random.uniform(jax.random.fold_in(jax.random.fold_in(own_key, 6), position), (shards_of,), jnp.float32, low / len(pieces), high / len(pieces))
        factor_of = factor_of * jnp.repeat(jnp.exp(steps), extent[position] // shards_of).reshape((-1,) + (1,) * (len(extent) - 1 - position))
    return factor_of


def profile(number_of, total, reach, skew):
    loads = [(1 << 20) // math.isqrt(standing ** skew) + 1 for standing in range(2, number_of + 1)]
    surplus, counts = total - reach - (number_of - 1), [1] * (number_of - 1)
    while surplus > 0:
        candidates = [i for i in range(number_of - 1) if counts[i] < reach]
        pool, left = sum([loads[i] for i in candidates]), surplus
        for i in candidates:
            extra = min(reach - counts[i], max(1, left * loads[i] // pool), surplus)
            counts[i] = counts[i] + extra
            surplus = surplus - extra
    return np.array([reach] + counts)


def ragged(rng, number_of, total, bound, skew):
    if number_of == 2:
        one = jax.random.randint(rng, (), max(1, total - bound), min(bound, total - 1) + 1)
        return jnp.stack([one, total - one])
    sizes = jnp.asarray(profile(number_of, total, bound, skew), jnp.int32)
    twos = (number_of - 1) // 2
    donor, sink = sizes[1:1 + 2 * twos:2], sizes[2:2 + 2 * twos:2]
    margin = jnp.minimum(donor - 1, bound - sink)
    moved = jax.random.randint(jax.random.fold_in(rng, 1), (twos,), 0, 1 << 20) % (margin + 1)
    sizes = sizes.at[1:1 + 2 * twos:2].set(donor - moved).at[2:2 + 2 * twos:2].set(sink + moved)
    return sizes[jax.random.permutation(jax.random.fold_in(rng, 2), number_of)]


def gaussian(rng, extent, scale, most, cuts=(), kind=jnp.bfloat16):
    factor_of = levels(rng, extent, cuts, -0.22, 0.18) if cuts else 1.0
    entries = jax.random.normal(rng, extent, jnp.float32) * scale * factor_of
    return jnp.minimum(jnp.maximum(entries, -most), most).astype(kind)


def setup_inputs(seed: int = 0) -> dict:
    key_list = jax.random.split(jax.random.key(seed), 5)
    queries = draw_queries(jax.random.fold_in(key_list[4], 71), 0)
    pairs = draw_pairs(jax.random.fold_in(key_list[4], 71), 0)
    out_proj = gaussian(key_list[2], (MBATCH, KVH, GROUP * HD, D), (HEADS * HD // 64) ** -0.5, 0.625, ((0, 4), (1, 2)))
    lengths = jax.vmap(lambda own: ragged(own, ROLLS, SEQ, SEQ // 2, 2))(jax.random.split(key_list[3], MBATCH)).reshape((MBATCH, ROLLS)).astype(jnp.int32)
    return dict(queries=queries, pairs=pairs, out_proj=out_proj, lengths=lengths)


def rollout_ids(positions, row_lengths):
    row_ends = jnp.cumsum(row_lengths).astype(jnp.int32)
    return lax.optimization_barrier(jnp.sum((positions[:, None] >= row_ends[None, :]).astype(jnp.int32), axis=1)).astype(jnp.int32)

def attend_batch(query_rows, pair_rows, row_lengths):
    seq_len = query_rows.shape[0]
    head_dim = pair_rows.shape[2] // 2
    kv_heads = pair_rows.shape[1]
    group_size = query_rows.shape[2] // head_dim
    block_rows = math.gcd(seq_len, 512)
    positions = jnp.arange(seq_len, dtype=jnp.int32)
    rollout = rollout_ids(positions, row_lengths)
    key_rows = pair_rows[:, :, :head_dim].astype(jnp.float32)
    value_rows = pair_rows[:, :, head_dim:].astype(jnp.float32)
    score_scale = 1.0 / math.sqrt(head_dim)

    def one_block(block_index):
        begin = (block_index * block_rows).astype(jnp.int32)
        query_block = lax.dynamic_slice_in_dim(query_rows, begin, block_rows, 0)
        query_block = query_block.astype(jnp.float32).reshape(block_rows, kv_heads, group_size, head_dim)
        row_pos = begin + jnp.arange(block_rows, dtype=jnp.int32)
        row_rollout = lax.dynamic_slice_in_dim(rollout, begin, block_rows, 0)
        scores = jnp.einsum('rhgd,khd->hgrk', query_block, key_rows) * score_scale
        visible = (row_rollout[:, None] == rollout[None, :]) & (positions[None, :] <= row_pos[:, None])
        scores = jnp.where(visible, scores, -1e+30)
        row_peak = lax.optimization_barrier(jnp.max(scores, axis=-1, keepdims=True))
        weights = jnp.where(visible, jnp.exp(scores - row_peak), 0.0)
        denom = lax.optimization_barrier(jnp.sum(weights, axis=-1))
        probs = lax.optimization_barrier(weights.astype(jnp.bfloat16)).astype(jnp.float32)
        outputs = jnp.einsum('hgrk,khd->hgrd', probs, value_rows) / denom[..., None]
        return jnp.transpose(outputs, (2, 0, 1, 3)).reshape(block_rows, kv_heads, group_size * head_dim)
    blocks = lax.map(one_block, jnp.arange(seq_len // block_rows, dtype=jnp.int32))
    return blocks.reshape(seq_len, kv_heads, group_size * head_dim).astype(jnp.bfloat16)

def reference(queries, pairs, out_proj, lengths):

    def one_section(section):
        batch_index = ((section + 1) % MBATCH).astype(jnp.int32)
        attended = attend_batch(queries[batch_index], pairs[batch_index], lengths[batch_index])
        head_parts = attended.reshape(SEQ, N_TP, -1)
        weight_parts = out_proj[section].reshape(N_TP, -1, D)
        summed = jnp.zeros((SEQ, D), jnp.float32)
        for group_index in range(N_TP):
            partial_sum = jnp.dot(head_parts[:, group_index], weight_parts[group_index], preferred_element_type=jnp.float32)
            summed = summed + lax.optimization_barrier(partial_sum.astype(jnp.bfloat16)).astype(jnp.float32)
        return summed.astype(jnp.bfloat16)
    return lax.map(one_section, jnp.arange(MBATCH, dtype=jnp.int32))
```

```python
import functools
import math

import jax
import jax.numpy as jnp
from jax import lax
from jax.experimental import pallas as pl
from jax.experimental.pallas import tpu as pltpu
from jax.sharding import PartitionSpec as P

MESH = pl.DeviceIdType.MESH
HIDDEN = -1e30


def tile_of(columns):
    for tile in (512, 256, 128):
        if columns % tile == 0:
            return tile
    return columns


def kernel(
    sizes,
    lengths_ref,
    q_hbm,
    kv_hbm,
    w_hbm,
    out_ref,
    q_ref,
    kv_ref,
    w_ref,
    seen_ref,
    hide_ref,
    sent_ref,
    got_ref,
    acc_ref,
    part_ref,
    share_ref,
    q_sem,
    kv_sem,
    w_sem,
    seen_send,
    seen_recv,
    att_send,
    att_recv,
    share_send,
    share_recv,
):
    n_seg, n_ctx, n_tp, rows, heads, head_dim, group, back = sizes
    seg = lax.axis_index("segment")
    ctx = lax.axis_index("ctx")
    tp = lax.axis_index("tp")
    width = group * head_dim
    columns = out_ref.shape[1]
    tile = tile_of(columns)
    tiles = columns // tile
    depth = (back + 1) * rows

    kv_copy = pltpu.make_async_copy(kv_hbm, kv_ref, kv_sem)
    kv_copy.start()
    q_copy = pltpu.make_async_copy(q_hbm, q_ref, q_sem)
    q_copy.start()

    def w_copy(h):
        part = pl.ds(pl.multiple_of(h * width, width), width)
        return pltpu.make_async_copy(w_hbm.at[part], w_ref.at[part], w_sem.at[h])

    for h in range(heads):
        w_copy(h).start()

    barrier = pltpu.get_barrier_semaphore()
    greeted = jnp.int32(0)
    for by in range(1, back + 1):
        for peer in (ctx - by, ctx + by):
            valid = (peer >= 0) & (peer < n_ctx)
            greeted = greeted + valid.astype(jnp.int32)

            @pl.when(valid)
            def _():
                pl.semaphore_signal(
                    barrier, inc=1, device_id={"ctx": peer}, device_id_type=MESH
                )

    to_seg = lax.rem(seg + n_seg - 1, n_seg)
    from_seg = lax.rem(seg + 1, n_seg)
    for peer in (to_seg, from_seg):
        pl.semaphore_signal(
            barrier, inc=1, device_id={"segment": peer}, device_id_type=MESH
        )
    for by in range(1, n_tp):
        pl.semaphore_signal(
            barrier,
            inc=1,
            device_id={"tp": lax.rem(tp + by, n_tp)},
            device_id_type=MESH,
        )
    pl.semaphore_wait(barrier, greeted + 2 + n_tp - 1)

    def kv_send(by, h):
        part = pl.ds(pl.multiple_of(h * 2 * head_dim, 2 * head_dim), 2 * head_dim)
        return pltpu.make_async_remote_copy(
            src_ref=kv_ref.at[:, part],
            dst_ref=seen_ref.at[by - 1, :, part],
            send_sem=seen_send.at[by - 1, h],
            recv_sem=seen_recv.at[by - 1, h],
            device_id={"ctx": lax.rem(ctx + by, n_ctx)},
            device_id_type=MESH,
        )

    kv_copy.wait()
    for h in range(heads):
        for by in range(1, back + 1):

            @pl.when(ctx + by < n_ctx)
            def _():
                kv_send(by, h).start()

    for by in range(1, back + 1):

        @pl.when(ctx < by)
        def _():
            seen_ref[by - 1] = jnp.zeros(seen_ref.shape[1:], seen_ref.dtype)

    query_pos = ctx * rows + lax.broadcasted_iota(jnp.int32, (rows, depth), 0)
    key_pos = (ctx - back) * rows + lax.broadcasted_iota(jnp.int32, (rows, depth), 1)
    first = jnp.zeros((rows, depth), jnp.int32)
    end = jnp.int32(0)
    for k in range(lengths_ref.shape[1]):
        end = end + lengths_ref[seg, k]
        first = jnp.where(query_pos >= end, end, first)
    visible = (key_pos >= first) & (key_pos <= query_pos)
    hide_ref[...] = jnp.where(visible, 0.0, HIDDEN)
    acc_ref[...] = jnp.zeros_like(acc_ref)
    q_copy.wait()

    factor = math.log2(math.e) / math.sqrt(head_dim)

    def att_copy(h):
        return pltpu.make_async_remote_copy(
            src_ref=sent_ref.at[h],
            dst_ref=got_ref.at[h],
            send_sem=att_send.at[h],
            recv_sem=att_recv.at[h],
            device_id={"segment": to_seg},
            device_id_type=MESH,
        )

    def attend(h, carry):
        for by in range(1, back + 1):

            @pl.when(ctx >= by)
            def _():
                kv_send(by, h).wait_recv()

        key_part = pl.ds(pl.multiple_of(h * 2 * head_dim, head_dim), head_dim)
        value_part = pl.ds(
            pl.multiple_of(h * 2 * head_dim + head_dim, head_dim), head_dim
        )
        blocks = [seen_ref.at[by - 1] for by in range(back, 0, -1)] + [kv_ref]
        keys = jnp.concatenate([block[:, key_part] for block in blocks], axis=0)
        values = jnp.concatenate([block[:, value_part] for block in blocks], axis=0)
        for g in range(group):
            at = pl.ds(pl.multiple_of((h * group + g) * head_dim, head_dim), head_dim)
            scores = lax.dot_general(
                q_ref[:, at],
                keys,
                (((1,), (1,)), ((), ())),
                preferred_element_type=jnp.float32,
            )
            scores = scores + hide_ref[...]
            peak = jnp.max(scores, axis=1, keepdims=True)
            weights = jnp.exp2((scores - peak) * factor)
            denom = jnp.sum(weights, axis=1, keepdims=True)
            mixed = jnp.dot(
                weights.astype(jnp.bfloat16), values, preferred_element_type=jnp.float32
            )
            sent_ref[h, :, g * head_dim : (g + 1) * head_dim] = (mixed / denom).astype(
                jnp.bfloat16
            )
        att_copy(h).start()
        return carry

    lax.fori_loop(0, heads, attend, 0)

    def w_part(h, begin):
        return w_ref[
            pl.ds(pl.multiple_of(h * width, width), width),
            pl.ds(pl.multiple_of(begin, tile), tile),
        ]

    def total_of(h, begin):
        return acc_ref[:, pl.ds(pl.multiple_of(begin, tile), tile)] + jnp.dot(
            got_ref[h], w_part(h, begin), preferred_element_type=jnp.float32
        )

    def project(h, carry):
        w_copy(h).wait()
        att_copy(h).wait_recv()

        def one(n, inner):
            begin = n * tile
            acc_ref[:, pl.ds(pl.multiple_of(begin, tile), tile)] = total_of(h, begin)
            return inner

        return lax.fori_loop(0, n_tp * tiles, one, carry)

    last = heads - 1
    lax.fori_loop(0, last, project, 0)
    w_copy(last).wait()
    att_copy(last).wait_recv()

    def share_copy(by, n):
        at = pl.ds(pl.multiple_of(n * tile, tile), tile)
        return pltpu.make_async_remote_copy(
            src_ref=part_ref.at[by - 1, :, at],
            dst_ref=share_ref.at[by - 1, :, at],
            send_sem=share_send.at[by - 1, n],
            recv_sem=share_recv.at[by - 1, n],
            device_id={"tp": lax.rem(tp + by, n_tp)},
            device_id_type=MESH,
        )

    for by in range(1, n_tp):
        peer = lax.rem(tp + by, n_tp)

        def theirs(n, inner):
            at = pl.ds(pl.multiple_of(n * tile, tile), tile)
            part_ref[by - 1, :, at] = total_of(last, peer * columns + n * tile).astype(
                jnp.bfloat16
            )
            share_copy(by, n).start()
            return inner

        lax.fori_loop(0, tiles, theirs, 0)

    def ours(n, inner):
        total = total_of(last, tp * columns + n * tile)
        at = pl.ds(pl.multiple_of(n * tile, tile), tile)
        for by in range(1, n_tp):
            share_copy(by, n).wait_recv()
            total = total + share_ref[by - 1, :, at].astype(jnp.float32)
        out_ref[:, at] = total.astype(jnp.bfloat16)
        return inner

    lax.fori_loop(0, tiles, ours, 0)

    for h in range(heads):
        att_copy(h).wait_send()
        for by in range(1, back + 1):

            @pl.when(ctx + by < n_ctx)
            def _():
                kv_send(by, h).wait_send()

    for by in range(1, n_tp):
        for n in range(tiles):
            share_copy(by, n).wait_send()


def local(n_seg, n_ctx, n_tp, queries, pairs, out_proj, lengths):
    rows, heads = pairs.shape[1], pairs.shape[2]
    head_dim = pairs.shape[3] // 2
    width = queries.shape[3]
    group = width // head_dim
    model = out_proj.shape[3]
    columns = model // n_tp
    back = min(n_ctx - 1, -(-(rows * n_ctx // 2 - 1) // rows))
    tiles = columns // tile_of(columns)
    sizes = (n_seg, n_ctx, n_tp, rows, heads, head_dim, group, back)
    bf16 = jnp.bfloat16
    dma = pltpu.SemaphoreType.DMA
    result = pl.pallas_call(
        functools.partial(kernel, sizes),
        out_shape=jax.ShapeDtypeStruct((rows, columns), bf16),
        in_specs=[pl.BlockSpec(memory_space=pltpu.SMEM)]
        + [pl.BlockSpec(memory_space=pl.ANY)] * 3,
        out_specs=pl.BlockSpec(memory_space=pltpu.VMEM),
        scratch_shapes=[
            pltpu.VMEM((rows, heads * width), bf16),
            pltpu.VMEM((rows, heads * 2 * head_dim), bf16),
            pltpu.VMEM((heads * width, model), bf16),
            pltpu.VMEM((back, rows, heads * 2 * head_dim), bf16),
            pltpu.VMEM((rows, (back + 1) * rows), jnp.float32),
            pltpu.VMEM((heads, rows, width), bf16),
            pltpu.VMEM((heads, rows, width), bf16),
            pltpu.VMEM((rows, model), jnp.float32),
            pltpu.VMEM((n_tp - 1, rows, columns), bf16),
            pltpu.VMEM((n_tp - 1, rows, columns), bf16),
            dma,
            dma,
            dma((heads,)),
            dma((back, heads)),
            dma((back, heads)),
            dma((heads,)),
            dma((heads,)),
            dma((n_tp - 1, tiles)),
            dma((n_tp - 1, tiles)),
        ],
        compiler_params=pltpu.CompilerParams(
            collective_id=0, has_side_effects=True, vmem_limit_bytes=60 << 20
        ),
    )(
        lengths,
        queries.reshape(rows, heads * width),
        pairs.reshape(rows, heads * 2 * head_dim),
        out_proj.reshape(heads * width, model),
    )
    return result.reshape(1, rows, columns)


def solution(mesh):
    sizes = [mesh.shape[axis] for axis in ("segment", "ctx", "tp")]
    return jax.shard_map(
        functools.partial(local, *sizes),
        mesh=mesh,
        in_specs=(
            P("segment", "ctx", "tp", None),
            P("segment", "ctx", "tp", None),
            P("segment", "tp", None, None),
            P(),
        ),
        out_specs=P("segment", "ctx", "tp"),
        check_vma=False,
    )
```

```python
import functools
import math

import jax
import jax.numpy as jnp
from jax import lax
from jax.experimental import pallas as pl
from jax.experimental.pallas import tpu as pltpu
from jax.sharding import PartitionSpec as P

MESH = pl.DeviceIdType.MESH
HIDDEN = -1e30


def tile_of(columns):
    for tile in (512, 256, 128):
        if columns % tile == 0:
            return tile
    return columns


def kernel(
    sizes,
    lengths_ref,
    q_hbm,
    kv_hbm,
    w_hbm,
    out_ref,
    q_ref,
    kv_ref,
    w_ref,
    seen_ref,
    hide_ref,
    sent_ref,
    got_ref,
    acc_ref,
    part_ref,
    share_ref,
    q_sem,
    kv_sem,
    w_sem,
    seen_send,
    seen_recv,
    att_send,
    att_recv,
    share_send,
    share_recv,
):
    n_seg, n_ctx, n_tp, rows, heads, head_dim, group, back = sizes
    seg = lax.axis_index("segment")
    ctx = lax.axis_index("ctx")
    tp = lax.axis_index("tp")
    width = group * head_dim
    columns = out_ref.shape[1]
    tile = tile_of(columns)
    tiles = columns // tile
    depth = (back + 1) * rows

    kv_copy = pltpu.make_async_copy(kv_hbm, kv_ref, kv_sem)
    kv_copy.start()
    q_copy = pltpu.make_async_copy(q_hbm, q_ref, q_sem)
    q_copy.start()

    def w_copy(h):
        part = pl.ds(pl.multiple_of(h * width, width), width)
        return pltpu.make_async_copy(w_hbm.at[part], w_ref.at[part], w_sem.at[h])

    for h in range(heads):
        w_copy(h).start()

    barrier = pltpu.get_barrier_semaphore()
    greeted = jnp.int32(0)
    for by in range(1, back + 1):
        for peer in (ctx - by, ctx + by):
            valid = (peer >= 0) & (peer < n_ctx)
            greeted = greeted + valid.astype(jnp.int32)

            @pl.when(valid)
            def _():
                pl.semaphore_signal(
                    barrier, inc=1, device_id={"ctx": peer}, device_id_type=MESH
                )

    to_seg = lax.rem(seg + n_seg - 1, n_seg)
    from_seg = lax.rem(seg + 1, n_seg)
    for peer in (to_seg, from_seg):
        pl.semaphore_signal(
            barrier, inc=1, device_id={"segment": peer}, device_id_type=MESH
        )
    for by in range(1, n_tp):
        pl.semaphore_signal(
            barrier,
            inc=1,
            device_id={"tp": lax.rem(tp + by, n_tp)},
            device_id_type=MESH,
        )
    pl.semaphore_wait(barrier, greeted + 2 + n_tp - 1)

    def kv_send(by, h):
        part = pl.ds(pl.multiple_of(h * 2 * head_dim, 2 * head_dim), 2 * head_dim)
        return pltpu.make_async_remote_copy(
            src_ref=kv_ref.at[:, part],
            dst_ref=seen_ref.at[by - 1, :, part],
            send_sem=seen_send.at[by - 1, h],
            recv_sem=seen_recv.at[by - 1, h],
            device_id={"ctx": lax.rem(ctx + by, n_ctx)},
            device_id_type=MESH,
        )

    relayed = n_ctx == 4 and back == 2

    def direct(by):
        sends = ctx + by < n_ctx
        return sends & (ctx != 1) if relayed and by == 1 else sends

    def relay(h):
        part = pl.ds(pl.multiple_of(h * 2 * head_dim, 2 * head_dim), 2 * head_dim)
        return pltpu.make_async_remote_copy(
            src_ref=seen_ref.at[1, :, part],
            dst_ref=seen_ref.at[0, :, part],
            send_sem=seen_send.at[0, h],
            recv_sem=seen_recv.at[0, h],
            device_id={"ctx": 2},
            device_id_type=MESH,
        )

    kv_copy.wait()
    for h in range(heads):
        for by in range(1, back + 1):

            @pl.when(direct(by))
            def _():
                kv_send(by, h).start()

    for by in range(1, back + 1):

        @pl.when(ctx < by)
        def _():
            seen_ref[by - 1] = jnp.zeros(seen_ref.shape[1:], seen_ref.dtype)

    query_pos = ctx * rows + lax.broadcasted_iota(jnp.int32, (rows, depth), 0)
    key_pos = (ctx - back) * rows + lax.broadcasted_iota(jnp.int32, (rows, depth), 1)
    first = jnp.zeros((rows, depth), jnp.int32)
    end = jnp.int32(0)
    for k in range(lengths_ref.shape[1]):
        end = end + lengths_ref[seg, k]
        first = jnp.where(query_pos >= end, end, first)
    visible = (key_pos >= first) & (key_pos <= query_pos)
    hide_ref[...] = jnp.where(visible, 0.0, HIDDEN)
    acc_ref[...] = jnp.zeros_like(acc_ref)
    q_copy.wait()

    factor = math.log2(math.e) / math.sqrt(head_dim)

    def att_copy(h):
        return pltpu.make_async_remote_copy(
            src_ref=sent_ref.at[h],
            dst_ref=got_ref.at[h],
            send_sem=att_send.at[h],
            recv_sem=att_recv.at[h],
            device_id={"segment": to_seg},
            device_id_type=MESH,
        )

    def attend(h, carry):
        for by in range(back, 0, -1):

            @pl.when(ctx >= by)
            def _():
                kv_send(by, h).wait_recv()

            if relayed and by == 2:

                @pl.when(ctx == 3)
                def _():
                    relay(h).start()

        key_part = pl.ds(pl.multiple_of(h * 2 * head_dim, head_dim), head_dim)
        value_part = pl.ds(
            pl.multiple_of(h * 2 * head_dim + head_dim, head_dim), head_dim
        )
        blocks = [seen_ref.at[by - 1] for by in range(back, 0, -1)] + [kv_ref]
        keys = jnp.concatenate([block[:, key_part] for block in blocks], axis=0)
        values = jnp.concatenate([block[:, value_part] for block in blocks], axis=0)
        for g in range(group):
            at = pl.ds(pl.multiple_of((h * group + g) * head_dim, head_dim), head_dim)
            scores = lax.dot_general(
                q_ref[:, at],
                keys,
                (((1,), (1,)), ((), ())),
                preferred_element_type=jnp.float32,
            )
            scores = scores + hide_ref[...]
            peak = jnp.max(scores, axis=1, keepdims=True)
            weights = jnp.exp2((scores - peak) * factor)
            denom = jnp.sum(weights, axis=1, keepdims=True)
            mixed = jnp.dot(
                weights.astype(jnp.bfloat16), values, preferred_element_type=jnp.float32
            )
            sent_ref[h, :, g * head_dim : (g + 1) * head_dim] = (mixed / denom).astype(
                jnp.bfloat16
            )
        att_copy(h).start()
        return carry

    lax.fori_loop(0, heads, attend, 0)

    def w_part(h, begin):
        return w_ref[
            pl.ds(pl.multiple_of(h * width, width), width),
            pl.ds(pl.multiple_of(begin, tile), tile),
        ]

    def total_of(h, begin):
        return acc_ref[:, pl.ds(pl.multiple_of(begin, tile), tile)] + jnp.dot(
            got_ref[h], w_part(h, begin), preferred_element_type=jnp.float32
        )

    def project(h, carry):
        w_copy(h).wait()
        att_copy(h).wait_recv()

        def one(n, inner):
            begin = n * tile
            acc_ref[:, pl.ds(pl.multiple_of(begin, tile), tile)] = total_of(h, begin)
            return inner

        return lax.fori_loop(0, n_tp * tiles, one, carry)

    last = heads - 1
    lax.fori_loop(0, last, project, 0)
    w_copy(last).wait()
    att_copy(last).wait_recv()

    def share_copy(by, n):
        at = pl.ds(pl.multiple_of(n * tile, tile), tile)
        return pltpu.make_async_remote_copy(
            src_ref=part_ref.at[by - 1, :, at],
            dst_ref=share_ref.at[by - 1, :, at],
            send_sem=share_send.at[by - 1, n],
            recv_sem=share_recv.at[by - 1, n],
            device_id={"tp": lax.rem(tp + by, n_tp)},
            device_id_type=MESH,
        )

    for by in range(1, n_tp):
        peer = lax.rem(tp + by, n_tp)

        def theirs(n, inner):
            at = pl.ds(pl.multiple_of(n * tile, tile), tile)
            part_ref[by - 1, :, at] = total_of(last, peer * columns + n * tile).astype(
                jnp.bfloat16
            )
            share_copy(by, n).start()
            return inner

        lax.fori_loop(0, tiles, theirs, 0)

    def ours(n, inner):
        total = total_of(last, tp * columns + n * tile)
        at = pl.ds(pl.multiple_of(n * tile, tile), tile)
        for by in range(1, n_tp):
            share_copy(by, n).wait_recv()
            total = total + share_ref[by - 1, :, at].astype(jnp.float32)
        out_ref[:, at] = total.astype(jnp.bfloat16)
        return inner

    lax.fori_loop(0, tiles, ours, 0)

    for h in range(heads):
        att_copy(h).wait_send()
        for by in range(1, back + 1):

            @pl.when(direct(by))
            def _():
                kv_send(by, h).wait_send()

        if relayed:

            @pl.when(ctx == 3)
            def _():
                relay(h).wait_send()

    for by in range(1, n_tp):
        for n in range(tiles):
            share_copy(by, n).wait_send()


def local(n_seg, n_ctx, n_tp, queries, pairs, out_proj, lengths):
    rows, heads = pairs.shape[1], pairs.shape[2]
    head_dim = pairs.shape[3] // 2
    width = queries.shape[3]
    group = width // head_dim
    model = out_proj.shape[3]
    columns = model // n_tp
    back = min(n_ctx - 1, -(-(rows * n_ctx // 2 - 1) // rows))
    tiles = columns // tile_of(columns)
    sizes = (n_seg, n_ctx, n_tp, rows, heads, head_dim, group, back)
    bf16 = jnp.bfloat16
    dma = pltpu.SemaphoreType.DMA
    result = pl.pallas_call(
        functools.partial(kernel, sizes),
        out_shape=jax.ShapeDtypeStruct((rows, columns), bf16),
        in_specs=[pl.BlockSpec(memory_space=pltpu.SMEM)]
        + [pl.BlockSpec(memory_space=pl.ANY)] * 3,
        out_specs=pl.BlockSpec(memory_space=pltpu.VMEM),
        scratch_shapes=[
            pltpu.VMEM((rows, heads * width), bf16),
            pltpu.VMEM((rows, heads * 2 * head_dim), bf16),
            pltpu.VMEM((heads * width, model), bf16),
            pltpu.VMEM((back, rows, heads * 2 * head_dim), bf16),
            pltpu.VMEM((rows, (back + 1) * rows), jnp.float32),
            pltpu.VMEM((heads, rows, width), bf16),
            pltpu.VMEM((heads, rows, width), bf16),
            pltpu.VMEM((rows, model), jnp.float32),
            pltpu.VMEM((n_tp - 1, rows, columns), bf16),
            pltpu.VMEM((n_tp - 1, rows, columns), bf16),
            dma,
            dma,
            dma((heads,)),
            dma((back, heads)),
            dma((back, heads)),
            dma((heads,)),
            dma((heads,)),
            dma((n_tp - 1, tiles)),
            dma((n_tp - 1, tiles)),
        ],
        compiler_params=pltpu.CompilerParams(
            collective_id=0, has_side_effects=True, vmem_limit_bytes=40 << 20
        ),
    )(
        lengths,
        queries.reshape(rows, heads * width),
        pairs.reshape(rows, heads * 2 * head_dim),
        out_proj.reshape(heads * width, model),
    )
    return result.reshape(1, rows, columns)


def solution(mesh):
    sizes = [mesh.shape[axis] for axis in ("segment", "ctx", "tp")]
    return jax.shard_map(
        functools.partial(local, *sizes),
        mesh=mesh,
        in_specs=(
            P("segment", "ctx", "tp", None),
            P("segment", "ctx", "tp", None),
            P("segment", "tp", None, None),
            P(),
        ),
        out_specs=P("segment", "ctx", "tp"),
        check_vma=False,
    )
```

```python
import functools
import math

import jax
import jax.numpy as jnp
from jax import lax
from jax.experimental import pallas as pl
from jax.experimental.pallas import tpu as pltpu
from jax.sharding import PartitionSpec as P

MESH = pl.DeviceIdType.MESH
HIDDEN = -1e30


def tile_of(columns):
    for tile in (1280, 640, 512, 256, 128):
        if columns % tile == 0:
            return tile
    return columns


def kernel(
    sizes,
    lengths_hbm,
    q_ref,
    kv_ref,
    w_hbm,
    out_ref,
    lengths_ref,
    w_ref,
    seen_ref,
    hide_ref,
    sent_ref,
    got_ref,
    acc_ref,
    part_ref,
    share_ref,
    lengths_sem,
    w_sem,
    seen_send,
    seen_recv,
    att_send,
    att_recv,
    share_send,
    share_recv,
):
    n_seg, n_ctx, n_tp, rows, heads, head_dim, group, back = sizes
    seg = lax.axis_index("segment")
    ctx = lax.axis_index("ctx")
    tp = lax.axis_index("tp")
    width = group * head_dim
    columns = out_ref.shape[1]
    tile = tile_of(columns)
    tiles = columns // tile
    depth = (back + 1) * rows

    lengths_copy = pltpu.make_async_copy(lengths_hbm, lengths_ref, lengths_sem)
    lengths_copy.start()

    def w_copy(h):
        part = pl.ds(pl.multiple_of(h * width, width), width)
        return pltpu.make_async_copy(w_hbm.at[part], w_ref.at[part], w_sem.at[h])

    for h in range(heads):
        w_copy(h).start()

    barrier = pltpu.get_barrier_semaphore()
    greeted = jnp.int32(0)
    for by in range(1, back + 1):
        for peer in (ctx - by, ctx + by):
            valid = (peer >= 0) & (peer < n_ctx)
            greeted = greeted + valid.astype(jnp.int32)

            @pl.when(valid)
            def _():
                pl.semaphore_signal(
                    barrier, inc=1, device_id={"ctx": peer}, device_id_type=MESH
                )

    to_seg = lax.rem(seg + n_seg - 1, n_seg)
    from_seg = lax.rem(seg + 1, n_seg)
    for peer in (to_seg, from_seg):
        pl.semaphore_signal(
            barrier, inc=1, device_id={"segment": peer}, device_id_type=MESH
        )
    for by in range(1, n_tp):
        pl.semaphore_signal(
            barrier,
            inc=1,
            device_id={"tp": lax.rem(tp + by, n_tp)},
            device_id_type=MESH,
        )
    pl.semaphore_wait(barrier, greeted + 2 + n_tp - 1)

    def kv_send(by, h):
        part = pl.ds(pl.multiple_of(h * 2 * head_dim, 2 * head_dim), 2 * head_dim)
        return pltpu.make_async_remote_copy(
            src_ref=kv_ref.at[:, part],
            dst_ref=seen_ref.at[by - 1, :, part],
            send_sem=seen_send.at[by - 1, h],
            recv_sem=seen_recv.at[by - 1, h],
            device_id={"ctx": lax.rem(ctx + by, n_ctx)},
            device_id_type=MESH,
        )

    relayed = n_ctx == 4 and back == 2

    def direct(by):
        sends = ctx + by < n_ctx
        return sends & (ctx != 1) if relayed and by == 1 else sends

    def relay(h):
        part = pl.ds(pl.multiple_of(h * 2 * head_dim, 2 * head_dim), 2 * head_dim)
        return pltpu.make_async_remote_copy(
            src_ref=seen_ref.at[1, :, part],
            dst_ref=seen_ref.at[0, :, part],
            send_sem=seen_send.at[0, h],
            recv_sem=seen_recv.at[0, h],
            device_id={"ctx": 2},
            device_id_type=MESH,
        )

    for h in range(heads):
        for by in range(1, back + 1):

            @pl.when(direct(by))
            def _():
                kv_send(by, h).start()

    for by in range(1, back + 1):

        @pl.when(ctx < by)
        def _():
            seen_ref[by - 1] = jnp.zeros(seen_ref.shape[1:], seen_ref.dtype)

    lengths_copy.wait()
    query_pos = ctx * rows + lax.broadcasted_iota(jnp.int32, (rows, depth), 0)
    key_pos = (ctx - back) * rows + lax.broadcasted_iota(jnp.int32, (rows, depth), 1)
    first = jnp.zeros((rows, depth), jnp.int32)
    end = jnp.int32(0)
    for k in range(lengths_ref.shape[1]):
        end = end + lengths_ref[seg, k]
        first = jnp.where(query_pos >= end, end, first)
    visible = (key_pos >= first) & (key_pos <= query_pos)
    hide_ref[...] = jnp.where(visible, 0.0, HIDDEN)
    acc_ref[...] = jnp.zeros_like(acc_ref)

    factor = math.log2(math.e) / math.sqrt(head_dim)

    def att_copy(unit):
        return pltpu.make_async_remote_copy(
            src_ref=sent_ref.at[unit],
            dst_ref=got_ref.at[unit],
            send_sem=att_send.at[unit],
            recv_sem=att_recv.at[unit],
            device_id={"segment": to_seg},
            device_id_type=MESH,
        )

    def attend(h, carry):
        for by in range(back, 0, -1):

            @pl.when(ctx >= by)
            def _():
                kv_send(by, h).wait_recv()

            if relayed and by == 2:

                @pl.when(ctx == 3)
                def _():
                    relay(h).start()

        key_part = pl.ds(pl.multiple_of(h * 2 * head_dim, head_dim), head_dim)
        value_part = pl.ds(
            pl.multiple_of(h * 2 * head_dim + head_dim, head_dim), head_dim
        )
        blocks = [seen_ref.at[by - 1] for by in range(back, 0, -1)] + [kv_ref]
        keys = jnp.concatenate([block[:, key_part] for block in blocks], axis=0)
        values = jnp.concatenate([block[:, value_part] for block in blocks], axis=0)
        for g in range(group):
            at = pl.ds(pl.multiple_of((h * group + g) * head_dim, head_dim), head_dim)
            scores = lax.dot_general(
                q_ref[:, at],
                keys,
                (((1,), (1,)), ((), ())),
                preferred_element_type=jnp.float32,
            )
            scores = scores + hide_ref[...]
            peak = jnp.max(scores, axis=1, keepdims=True)
            weights = jnp.exp2((scores - peak) * factor)
            denom = jnp.sum(weights, axis=1, keepdims=True)
            mixed = jnp.dot(
                weights.astype(jnp.bfloat16), values, preferred_element_type=jnp.float32
            )
            sent_ref[h * group + g] = (mixed * (1.0 / denom)).astype(jnp.bfloat16)
            att_copy(h * group + g).start()
        return carry

    late = max(1, min(group - 1, 2))

    def total_of(h, begin, low, high, tile=tile):
        mixed = jnp.concatenate(
            [got_ref[h * group + g] for g in range(low, high)], axis=1
        )
        weight = w_ref[
            pl.ds(
                pl.multiple_of(h * width + low * head_dim, head_dim),
                (high - low) * head_dim,
            ),
            pl.ds(pl.multiple_of(begin, tile), tile),
        ]
        return acc_ref[:, pl.ds(pl.multiple_of(begin, tile), tile)] + jnp.dot(
            mixed, weight, preferred_element_type=jnp.float32
        )

    def project(h, low, high):
        for g in range(low, high):
            att_copy(h * group + g).wait_recv()

        def one(n, inner):
            begin = pl.multiple_of(n * columns, columns)
            acc_ref[:, pl.ds(begin, columns)] = total_of(h, begin, low, high, columns)
            return inner

        lax.fori_loop(0, n_tp, one, 0)

    def attend_and_project(h, carry):
        attend(h, 0)
        w_copy(h - 1).wait()
        project(h - 1, 0, group)
        return carry

    last = heads - 1
    attend(0, 0)
    lax.fori_loop(1, heads, attend_and_project, 0)
    w_copy(last).wait()
    project(last, 0, group - late)
    for g in range(group - late, group):
        att_copy(last * group + g).wait_recv()

    def share_copy(by, n):
        at = pl.ds(pl.multiple_of(n * tile, tile), tile)
        return pltpu.make_async_remote_copy(
            src_ref=part_ref.at[by - 1, :, at],
            dst_ref=share_ref.at[by - 1, :, at],
            send_sem=share_send.at[by - 1, n],
            recv_sem=share_recv.at[by - 1, n],
            device_id={"tp": lax.rem(tp + by, n_tp)},
            device_id_type=MESH,
        )

    for by in range(1, n_tp):
        peer = lax.rem(tp + by, n_tp)

        for n in range(tiles):
            at = pl.ds(pl.multiple_of(n * tile, tile), tile)
            part_ref[by - 1, :, at] = total_of(
                last, peer * columns + n * tile, group - late, group
            ).astype(jnp.bfloat16)
            share_copy(by, n).start()

    for n in range(tiles):
        total = total_of(last, tp * columns + n * tile, group - late, group)
        at = pl.ds(pl.multiple_of(n * tile, tile), tile)
        for by in range(1, n_tp):
            share_copy(by, n).wait_recv()
            total = total + share_ref[by - 1, :, at].astype(jnp.float32)
        out_ref[:, at] = total.astype(jnp.bfloat16)

    for unit in range(heads * group):
        att_copy(unit).wait_send()
    for h in range(heads):
        for by in range(1, back + 1):

            @pl.when(direct(by))
            def _():
                kv_send(by, h).wait_send()

        if relayed:

            @pl.when(ctx == 3)
            def _():
                relay(h).wait_send()

    for by in range(1, n_tp):
        for n in range(tiles):
            share_copy(by, n).wait_send()


def local(n_seg, n_ctx, n_tp, queries, pairs, out_proj, lengths):
    rows, heads = pairs.shape[1], pairs.shape[2]
    head_dim = pairs.shape[3] // 2
    width = queries.shape[3]
    group = width // head_dim
    model = out_proj.shape[3]
    columns = model // n_tp
    back = min(n_ctx - 1, -(-(rows * n_ctx // 2 - 1) // rows))
    tiles = columns // tile_of(columns)
    sizes = (n_seg, n_ctx, n_tp, rows, heads, head_dim, group, back)
    bf16 = jnp.bfloat16
    dma = pltpu.SemaphoreType.DMA
    result = pl.pallas_call(
        functools.partial(kernel, sizes),
        out_shape=jax.ShapeDtypeStruct((rows, columns), bf16),
        in_specs=[
            pl.BlockSpec(memory_space=pltpu.HBM),
            pl.BlockSpec(memory_space=pltpu.VMEM),
            pl.BlockSpec(memory_space=pltpu.VMEM),
            pl.BlockSpec(memory_space=pl.ANY),
        ],
        out_specs=pl.BlockSpec(memory_space=pltpu.VMEM),
        scratch_shapes=[
            pltpu.SMEM(lengths.shape, jnp.int32),
            pltpu.VMEM((heads * width, model), bf16),
            pltpu.VMEM((back, rows, heads * 2 * head_dim), bf16),
            pltpu.VMEM((rows, (back + 1) * rows), jnp.float32),
            pltpu.VMEM((heads * group, rows, head_dim), bf16),
            pltpu.VMEM((heads * group, rows, head_dim), bf16),
            pltpu.VMEM((rows, model), jnp.float32),
            pltpu.VMEM((n_tp - 1, rows, columns), bf16),
            pltpu.VMEM((n_tp - 1, rows, columns), bf16),
            dma,
            dma((heads,)),
            dma((back, heads)),
            dma((back, heads)),
            dma((heads * group,)),
            dma((heads * group,)),
            dma((n_tp - 1, tiles)),
            dma((n_tp - 1, tiles)),
        ],
        compiler_params=pltpu.CompilerParams(
            collective_id=0, has_side_effects=True, vmem_limit_bytes=40 << 20
        ),
    )(
        lengths,
        queries.reshape(rows, heads * width),
        pairs.reshape(rows, heads * 2 * head_dim),
        out_proj.reshape(heads * width, model),
    )
    return result.reshape(1, rows, columns)


def solution(mesh):
    sizes = [mesh.shape[axis] for axis in ("segment", "ctx", "tp")]
    return jax.shard_map(
        functools.partial(local, *sizes),
        mesh=mesh,
        in_specs=(
            P("segment", "ctx", "tp", None),
            P("segment", "ctx", "tp", None),
            P("segment", "tp", None, None),
            P(),
        ),
        out_specs=P("segment", "ctx", "tp"),
        check_vma=False,
    )
```

```python
import functools
import math

import jax
import jax.numpy as jnp
from jax import lax
from jax.experimental import pallas as pl
from jax.experimental.pallas import tpu as pltpu
from jax.sharding import PartitionSpec as P

MESH = pl.DeviceIdType.MESH
HIDDEN = -1e30


def tile_of(columns):
    for tile in (1280, 640, 512, 256, 128):
        if columns % tile == 0:
            return tile
    return columns


def kernel(
    sizes,
    lengths_hbm,
    q_ref,
    kv_ref,
    w_hbm,
    out_ref,
    lengths_ref,
    w_ref,
    seen_ref,
    hide_ref,
    sent_ref,
    got_ref,
    acc_ref,
    part_ref,
    share_ref,
    lengths_sem,
    w_sem,
    seen_send,
    seen_recv,
    att_send,
    att_recv,
    share_send,
    share_recv,
):
    n_seg, n_ctx, n_tp, rows, heads, head_dim, group, back = sizes
    seg = lax.axis_index("segment")
    ctx = lax.axis_index("ctx")
    tp = lax.axis_index("tp")
    width = group * head_dim
    columns = out_ref.shape[1]
    tile = tile_of(columns)
    tiles = columns // tile
    depth = (back + 1) * rows

    lengths_copy = pltpu.make_async_copy(lengths_hbm, lengths_ref, lengths_sem)
    lengths_copy.start()

    def w_copy(h):
        part = pl.ds(pl.multiple_of(h * width, width), width)
        return pltpu.make_async_copy(w_hbm.at[part], w_ref.at[part], w_sem.at[h])

    for h in range(heads):
        w_copy(h).start()

    barrier = pltpu.get_barrier_semaphore()
    greeted = jnp.int32(0)
    for by in range(1, back + 1):
        for peer in (ctx - by, ctx + by):
            valid = (peer >= 0) & (peer < n_ctx)
            greeted = greeted + valid.astype(jnp.int32)

            @pl.when(valid)
            def _():
                pl.semaphore_signal(
                    barrier, inc=1, device_id={"ctx": peer}, device_id_type=MESH
                )

    to_seg = lax.rem(seg + n_seg - 1, n_seg)
    from_seg = lax.rem(seg + 1, n_seg)
    for peer in (to_seg, from_seg):
        pl.semaphore_signal(
            barrier, inc=1, device_id={"segment": peer}, device_id_type=MESH
        )
    for by in range(1, n_tp):
        pl.semaphore_signal(
            barrier,
            inc=1,
            device_id={"tp": lax.rem(tp + by, n_tp)},
            device_id_type=MESH,
        )
    pl.semaphore_wait(barrier, greeted + 2 + n_tp - 1)

    def kv_send(by, h):
        part = pl.ds(pl.multiple_of(h * 2 * head_dim, 2 * head_dim), 2 * head_dim)
        return pltpu.make_async_remote_copy(
            src_ref=kv_ref.at[:, part],
            dst_ref=seen_ref.at[by - 1, :, part],
            send_sem=seen_send.at[by - 1, h],
            recv_sem=seen_recv.at[by - 1, h],
            device_id={"ctx": lax.rem(ctx + by, n_ctx)},
            device_id_type=MESH,
        )

    relayed = [h for h in range(heads) if h % 2 == 1] if n_ctx == 4 and back == 2 else []

    def direct(by, h):
        sends = ctx + by < n_ctx
        return sends & (ctx != 1) if by == 1 and h in relayed else sends

    def relay(h):
        part = pl.ds(pl.multiple_of(h * 2 * head_dim, 2 * head_dim), 2 * head_dim)
        return pltpu.make_async_remote_copy(
            src_ref=seen_ref.at[1, :, part],
            dst_ref=seen_ref.at[0, :, part],
            send_sem=seen_send.at[0, h],
            recv_sem=seen_recv.at[0, h],
            device_id={"ctx": 2},
            device_id_type=MESH,
        )

    for h in range(heads):
        for by in range(1, back + 1):

            @pl.when(direct(by, h))
            def _():
                kv_send(by, h).start()

    for by in range(1, back + 1):

        @pl.when(ctx < by)
        def _():
            seen_ref[by - 1] = jnp.zeros(seen_ref.shape[1:], seen_ref.dtype)

    lengths_copy.wait()
    query_pos = ctx * rows + lax.broadcasted_iota(jnp.int32, (rows, depth), 0)
    key_pos = (ctx - back) * rows + lax.broadcasted_iota(jnp.int32, (rows, depth), 1)
    first = jnp.zeros((rows, depth), jnp.int32)
    end = jnp.int32(0)
    for k in range(lengths_ref.shape[1]):
        end = end + lengths_ref[seg, k]
        first = jnp.where(query_pos >= end, end, first)
    visible = (key_pos >= first) & (key_pos <= query_pos)
    hide_ref[...] = jnp.where(visible, 0.0, HIDDEN)
    acc_ref[...] = jnp.zeros_like(acc_ref)

    factor = math.log2(math.e) / math.sqrt(head_dim)

    def att_copy(unit):
        return pltpu.make_async_remote_copy(
            src_ref=sent_ref.at[unit],
            dst_ref=got_ref.at[unit],
            send_sem=att_send.at[unit],
            recv_sem=att_recv.at[unit],
            device_id={"segment": to_seg},
            device_id_type=MESH,
        )

    def waits_here(h):
        here = jnp.bool_(True)
        for other in relayed:
            here = here & (h != other)
        return here

    def pass_on(h):
        @pl.when(ctx == 3)
        def _():
            kv_send(2, h).wait_recv()
            relay(h).start()

    def attend(h, carry):
        for by in range(back, 0, -1):

            known = ctx >= by
            if relayed and by == 2:
                known = known & ((ctx != 3) | waits_here(h))

            @pl.when(known)
            def _():
                kv_send(by, h).wait_recv()


        key_part = pl.ds(pl.multiple_of(h * 2 * head_dim, head_dim), head_dim)
        value_part = pl.ds(
            pl.multiple_of(h * 2 * head_dim + head_dim, head_dim), head_dim
        )
        blocks = [seen_ref.at[by - 1] for by in range(back, 0, -1)] + [kv_ref]
        keys = jnp.concatenate([block[:, key_part] for block in blocks], axis=0)
        values = jnp.concatenate([block[:, value_part] for block in blocks], axis=0)
        for g in range(group):
            at = pl.ds(pl.multiple_of((h * group + g) * head_dim, head_dim), head_dim)
            scores = lax.dot_general(
                q_ref[:, at],
                keys,
                (((1,), (1,)), ((), ())),
                preferred_element_type=jnp.float32,
            )
            scores = scores + hide_ref[...]
            peak = jnp.max(scores, axis=1, keepdims=True)
            weights = jnp.exp2((scores - peak) * factor)
            denom = jnp.sum(weights, axis=1, keepdims=True)
            mixed = jnp.dot(
                weights.astype(jnp.bfloat16), values, preferred_element_type=jnp.float32
            )
            sent_ref[h * group + g] = (mixed * (1.0 / denom)).astype(jnp.bfloat16)
            att_copy(h * group + g).start()
        return carry

    late = max(1, min(group - 1, 2))

    def total_of(h, begin, low, high, tile=tile):
        mixed = jnp.concatenate(
            [got_ref[h * group + g] for g in range(low, high)], axis=1
        )
        weight = w_ref[
            pl.ds(
                pl.multiple_of(h * width + low * head_dim, head_dim),
                (high - low) * head_dim,
            ),
            pl.ds(pl.multiple_of(begin, tile), tile),
        ]
        return acc_ref[:, pl.ds(pl.multiple_of(begin, tile), tile)] + jnp.dot(
            mixed, weight, preferred_element_type=jnp.float32
        )

    def project(h, low, high):
        for g in range(low, high):
            att_copy(h * group + g).wait_recv()

        def one(n, inner):
            begin = pl.multiple_of(n * columns, columns)
            acc_ref[:, pl.ds(begin, columns)] = total_of(h, begin, low, high, columns)
            return inner

        lax.fori_loop(0, n_tp, one, 0)

    def attend_and_project(h, carry):
        attend(h, 0)
        w_copy(h - 1).wait()
        project(h - 1, 0, group)
        return carry

    last = heads - 1
    for h in relayed:
        if h == 0:
            pass_on(h)
    attend(0, 0)
    for h in relayed:
        if h > 0:
            pass_on(h)
    lax.fori_loop(1, heads, attend_and_project, 0)
    w_copy(last).wait()
    project(last, 0, group - late)
    for g in range(group - late, group):
        att_copy(last * group + g).wait_recv()

    def share_copy(by, n):
        at = pl.ds(pl.multiple_of(n * tile, tile), tile)
        return pltpu.make_async_remote_copy(
            src_ref=part_ref.at[by - 1, :, at],
            dst_ref=share_ref.at[by - 1, :, at],
            send_sem=share_send.at[by - 1, n],
            recv_sem=share_recv.at[by - 1, n],
            device_id={"tp": lax.rem(tp + by, n_tp)},
            device_id_type=MESH,
        )

    for by in range(1, n_tp):
        peer = lax.rem(tp + by, n_tp)

        for n in range(tiles):
            at = pl.ds(pl.multiple_of(n * tile, tile), tile)
            part_ref[by - 1, :, at] = total_of(
                last, peer * columns + n * tile, group - late, group
            ).astype(jnp.bfloat16)
            share_copy(by, n).start()

    for n in range(tiles):
        total = total_of(last, tp * columns + n * tile, group - late, group)
        at = pl.ds(pl.multiple_of(n * tile, tile), tile)
        for by in range(1, n_tp):
            share_copy(by, n).wait_recv()
            total = total + share_ref[by - 1, :, at].astype(jnp.float32)
        out_ref[:, at] = total.astype(jnp.bfloat16)

    for unit in range(heads * group):
        att_copy(unit).wait_send()
    for h in range(heads):
        for by in range(1, back + 1):

            @pl.when(direct(by, h))
            def _():
                kv_send(by, h).wait_send()

        if h in relayed:

            @pl.when(ctx == 3)
            def _():
                relay(h).wait_send()

    for by in range(1, n_tp):
        for n in range(tiles):
            share_copy(by, n).wait_send()


def local(n_seg, n_ctx, n_tp, queries, pairs, out_proj, lengths):
    rows, heads = pairs.shape[1], pairs.shape[2]
    head_dim = pairs.shape[3] // 2
    width = queries.shape[3]
    group = width // head_dim
    model = out_proj.shape[3]
    columns = model // n_tp
    back = min(n_ctx - 1, -(-(rows * n_ctx // 2 - 1) // rows))
    tiles = columns // tile_of(columns)
    sizes = (n_seg, n_ctx, n_tp, rows, heads, head_dim, group, back)
    bf16 = jnp.bfloat16
    dma = pltpu.SemaphoreType.DMA
    result = pl.pallas_call(
        functools.partial(kernel, sizes),
        out_shape=jax.ShapeDtypeStruct((rows, columns), bf16),
        in_specs=[
            pl.BlockSpec(memory_space=pltpu.HBM),
            pl.BlockSpec(memory_space=pltpu.VMEM),
            pl.BlockSpec(memory_space=pltpu.VMEM),
            pl.BlockSpec(memory_space=pl.ANY),
        ],
        out_specs=pl.BlockSpec(memory_space=pltpu.VMEM),
        scratch_shapes=[
            pltpu.SMEM(lengths.shape, jnp.int32),
            pltpu.VMEM((heads * width, model), bf16),
            pltpu.VMEM((back, rows, heads * 2 * head_dim), bf16),
            pltpu.VMEM((rows, (back + 1) * rows), jnp.float32),
            pltpu.VMEM((heads * group, rows, head_dim), bf16),
            pltpu.VMEM((heads * group, rows, head_dim), bf16),
            pltpu.VMEM((rows, model), jnp.float32),
            pltpu.VMEM((n_tp - 1, rows, columns), bf16),
            pltpu.VMEM((n_tp - 1, rows, columns), bf16),
            dma,
            dma((heads,)),
            dma((back, heads)),
            dma((back, heads)),
            dma((heads * group,)),
            dma((heads * group,)),
            dma((n_tp - 1, tiles)),
            dma((n_tp - 1, tiles)),
        ],
        compiler_params=pltpu.CompilerParams(
            collective_id=0, has_side_effects=True, vmem_limit_bytes=40 << 20
        ),
    )(
        lengths,
        queries.reshape(rows, heads * width),
        pairs.reshape(rows, heads * 2 * head_dim),
        out_proj.reshape(heads * width, model),
    )
    return result.reshape(1, rows, columns)


def solution(mesh):
    sizes = [mesh.shape[axis] for axis in ("segment", "ctx", "tp")]
    return jax.shard_map(
        functools.partial(local, *sizes),
        mesh=mesh,
        in_specs=(
            P("segment", "ctx", "tp", None),
            P("segment", "ctx", "tp", None),
            P("segment", "tp", None, None),
            P(),
        ),
        out_specs=P("segment", "ctx", "tp"),
        check_vma=False,
    )
```

```python
import functools
import math

import jax
import jax.numpy as jnp
from jax import lax
from jax.experimental import pallas as pl
from jax.experimental.pallas import tpu as pltpu
from jax.sharding import PartitionSpec as P

MESH = pl.DeviceIdType.MESH
HIDDEN = -1e30


def tile_of(columns):
    for tile in (1280, 640, 512, 256, 128):
        if columns % tile == 0:
            return tile
    return columns


def kernel(
    sizes,
    lengths_hbm,
    q_ref,
    kv_ref,
    w_hbm,
    out_ref,
    lengths_ref,
    w_ref,
    seen_ref,
    hide_ref,
    sent_ref,
    got_ref,
    acc_ref,
    part_ref,
    share_ref,
    lengths_sem,
    w_sem,
    seen_send,
    seen_recv,
    att_send,
    att_recv,
    share_send,
    share_recv,
):
    n_seg, n_ctx, n_tp, rows, heads, head_dim, group, back = sizes
    seg = lax.axis_index("segment")
    ctx = lax.axis_index("ctx")
    tp = lax.axis_index("tp")
    width = group * head_dim
    columns = out_ref.shape[1]
    tile = tile_of(columns)
    tiles = columns // tile
    depth = (back + 1) * rows

    lengths_copy = pltpu.make_async_copy(lengths_hbm, lengths_ref, lengths_sem)
    lengths_copy.start()

    def w_copy(h):
        part = pl.ds(pl.multiple_of(h * width, width), width)
        return pltpu.make_async_copy(w_hbm.at[part], w_ref.at[part], w_sem.at[h])

    for h in range(heads):
        w_copy(h).start()

    barrier = pltpu.get_barrier_semaphore()
    greeted = jnp.int32(0)
    for by in range(1, back + 1):
        for peer in (ctx - by, ctx + by):
            valid = (peer >= 0) & (peer < n_ctx)
            greeted = greeted + valid.astype(jnp.int32)

            @pl.when(valid)
            def _():
                pl.semaphore_signal(
                    barrier, inc=1, device_id={"ctx": peer}, device_id_type=MESH
                )

    to_seg = lax.rem(seg + n_seg - 1, n_seg)
    from_seg = lax.rem(seg + 1, n_seg)
    for peer in (to_seg, from_seg):
        pl.semaphore_signal(
            barrier, inc=1, device_id={"segment": peer}, device_id_type=MESH
        )
    for by in range(1, n_tp):
        pl.semaphore_signal(
            barrier,
            inc=1,
            device_id={"tp": lax.rem(tp + by, n_tp)},
            device_id_type=MESH,
        )
    pl.semaphore_wait(barrier, greeted + 2 + n_tp - 1)

    def kv_send(by, h):
        part = pl.ds(pl.multiple_of(h * 2 * head_dim, 2 * head_dim), 2 * head_dim)
        return pltpu.make_async_remote_copy(
            src_ref=kv_ref.at[:, part],
            dst_ref=seen_ref.at[by - 1, :, part],
            send_sem=seen_send.at[by - 1, h],
            recv_sem=seen_recv.at[by - 1, h],
            device_id={"ctx": lax.rem(ctx + by, n_ctx)},
            device_id_type=MESH,
        )

    relayed = [h for h in range(heads) if h % 2 == 1] if n_ctx == 4 and back == 2 else []

    def direct(by, h):
        sends = ctx + by < n_ctx
        return sends & (ctx != 1) if by == 1 and h in relayed else sends

    def relay(h):
        part = pl.ds(pl.multiple_of(h * 2 * head_dim, 2 * head_dim), 2 * head_dim)
        return pltpu.make_async_remote_copy(
            src_ref=seen_ref.at[1, :, part],
            dst_ref=seen_ref.at[0, :, part],
            send_sem=seen_send.at[0, h],
            recv_sem=seen_recv.at[0, h],
            device_id={"ctx": 2},
            device_id_type=MESH,
        )

    for h in range(heads):
        for by in range(1, back + 1):

            @pl.when(direct(by, h))
            def _():
                kv_send(by, h).start()

    for by in range(1, back + 1):

        @pl.when(ctx < by)
        def _():
            seen_ref[by - 1] = jnp.zeros(seen_ref.shape[1:], seen_ref.dtype)

    lengths_copy.wait()
    query_pos = ctx * rows + lax.broadcasted_iota(jnp.int32, (rows, depth), 0)
    key_pos = (ctx - back) * rows + lax.broadcasted_iota(jnp.int32, (rows, depth), 1)
    first = jnp.zeros((rows, depth), jnp.int32)
    end = jnp.int32(0)
    for k in range(lengths_ref.shape[1]):
        end = end + lengths_ref[seg, k]
        first = jnp.where(query_pos >= end, end, first)
    visible = (key_pos >= first) & (key_pos <= query_pos)
    hide_ref[...] = jnp.where(visible, 0.0, HIDDEN)
    acc_ref[...] = jnp.zeros_like(acc_ref)

    factor = math.log2(math.e) / math.sqrt(head_dim)

    def att_copy(unit):
        return pltpu.make_async_remote_copy(
            src_ref=sent_ref.at[unit],
            dst_ref=got_ref.at[unit],
            send_sem=att_send.at[unit],
            recv_sem=att_recv.at[unit],
            device_id={"segment": to_seg},
            device_id_type=MESH,
        )

    def waits_here(h):
        here = jnp.bool_(True)
        for other in relayed:
            here = here & (h != other)
        return here

    def pass_on(h):
        @pl.when(ctx == 3)
        def _():
            kv_send(2, h).wait_recv()
            relay(h).start()

    def attend(h, carry):
        for by in range(back, 0, -1):

            known = ctx >= by
            if relayed and by == 2:
                known = known & ((ctx != 3) | waits_here(h))

            @pl.when(known)
            def _():
                kv_send(by, h).wait_recv()


        key_part = pl.ds(pl.multiple_of(h * 2 * head_dim, head_dim), head_dim)
        value_part = pl.ds(
            pl.multiple_of(h * 2 * head_dim + head_dim, head_dim), head_dim
        )
        blocks = [seen_ref.at[by - 1] for by in range(back, 0, -1)] + [kv_ref]
        keys = jnp.concatenate([block[:, key_part] for block in blocks], axis=0)
        values = jnp.concatenate([block[:, value_part] for block in blocks], axis=0)
        for g in range(group):
            at = pl.ds(pl.multiple_of((h * group + g) * head_dim, head_dim), head_dim)
            scores = lax.dot_general(
                q_ref[:, at],
                keys,
                (((1,), (1,)), ((), ())),
                preferred_element_type=jnp.float32,
            )
            scores = scores + hide_ref[...]
            peak = jnp.max(scores, axis=1, keepdims=True)
            weights = jnp.exp2((scores - peak) * factor)
            denom = jnp.sum(weights, axis=1, keepdims=True)
            mixed = jnp.dot(
                weights.astype(jnp.bfloat16), values, preferred_element_type=jnp.float32
            )
            sent_ref[h * group + g] = (mixed * (1.0 / denom)).astype(jnp.bfloat16)
            att_copy(h * group + g).start()
        return carry

    late = group

    def total_of(h, begin, low, high, tile=tile):
        mixed = jnp.concatenate(
            [got_ref[h * group + g] for g in range(low, high)], axis=1
        )
        weight = w_ref[
            pl.ds(
                pl.multiple_of(h * width + low * head_dim, head_dim),
                (high - low) * head_dim,
            ),
            pl.ds(pl.multiple_of(begin, tile), tile),
        ]
        return acc_ref[:, pl.ds(pl.multiple_of(begin, tile), tile)] + jnp.dot(
            mixed, weight, preferred_element_type=jnp.float32
        )

    def project(h, low, high):
        for g in range(low, high):
            att_copy(h * group + g).wait_recv()

        def one(n, inner):
            begin = pl.multiple_of(n * columns, columns)
            acc_ref[:, pl.ds(begin, columns)] = total_of(h, begin, low, high, columns)
            return inner

        lax.fori_loop(0, n_tp, one, 0)

    def attend_and_project(h, carry):
        attend(h, 0)
        w_copy(h - 1).wait()
        project(h - 1, 0, group)
        return carry

    last = heads - 1
    for h in relayed:
        if h == 0:
            pass_on(h)
    attend(0, 0)
    for h in relayed:
        if h > 0:
            pass_on(h)
    lax.fori_loop(1, heads, attend_and_project, 0)
    w_copy(last).wait()
    if late < group:
        project(last, 0, group - late)
    for g in range(group - late, group):
        att_copy(last * group + g).wait_recv()

    def share_copy(by, n):
        at = pl.ds(pl.multiple_of(n * tile, tile), tile)
        return pltpu.make_async_remote_copy(
            src_ref=part_ref.at[by - 1, :, at],
            dst_ref=share_ref.at[by - 1, :, at],
            send_sem=share_send.at[by - 1, n],
            recv_sem=share_recv.at[by - 1, n],
            device_id={"tp": lax.rem(tp + by, n_tp)},
            device_id_type=MESH,
        )

    for by in range(1, n_tp):
        peer = lax.rem(tp + by, n_tp)

        for n in range(tiles):
            at = pl.ds(pl.multiple_of(n * tile, tile), tile)
            part_ref[by - 1, :, at] = total_of(
                last, peer * columns + n * tile, group - late, group
            ).astype(jnp.bfloat16)
            share_copy(by, n).start()

    for n in range(tiles):
        total = total_of(last, tp * columns + n * tile, group - late, group)
        at = pl.ds(pl.multiple_of(n * tile, tile), tile)
        for by in range(1, n_tp):
            share_copy(by, n).wait_recv()
            total = total + share_ref[by - 1, :, at].astype(jnp.float32)
        out_ref[:, at] = total.astype(jnp.bfloat16)

    for unit in range(heads * group):
        att_copy(unit).wait_send()
    for h in range(heads):
        for by in range(1, back + 1):

            @pl.when(direct(by, h))
            def _():
                kv_send(by, h).wait_send()

        if h in relayed:

            @pl.when(ctx == 3)
            def _():
                relay(h).wait_send()

    for by in range(1, n_tp):
        for n in range(tiles):
            share_copy(by, n).wait_send()


def local(n_seg, n_ctx, n_tp, queries, pairs, out_proj, lengths):
    rows, heads = pairs.shape[1], pairs.shape[2]
    head_dim = pairs.shape[3] // 2
    width = queries.shape[3]
    group = width // head_dim
    model = out_proj.shape[3]
    columns = model // n_tp
    back = min(n_ctx - 1, -(-(rows * n_ctx // 2 - 1) // rows))
    tiles = columns // tile_of(columns)
    sizes = (n_seg, n_ctx, n_tp, rows, heads, head_dim, group, back)
    bf16 = jnp.bfloat16
    dma = pltpu.SemaphoreType.DMA
    result = pl.pallas_call(
        functools.partial(kernel, sizes),
        out_shape=jax.ShapeDtypeStruct((rows, columns), bf16),
        in_specs=[
            pl.BlockSpec(memory_space=pltpu.HBM),
            pl.BlockSpec(memory_space=pltpu.VMEM),
            pl.BlockSpec(memory_space=pltpu.VMEM),
            pl.BlockSpec(memory_space=pl.ANY),
        ],
        out_specs=pl.BlockSpec(memory_space=pltpu.VMEM),
        scratch_shapes=[
            pltpu.SMEM(lengths.shape, jnp.int32),
            pltpu.VMEM((heads * width, model), bf16),
            pltpu.VMEM((back, rows, heads * 2 * head_dim), bf16),
            pltpu.VMEM((rows, (back + 1) * rows), jnp.float32),
            pltpu.VMEM((heads * group, rows, head_dim), bf16),
            pltpu.VMEM((heads * group, rows, head_dim), bf16),
            pltpu.VMEM((rows, model), jnp.float32),
            pltpu.VMEM((n_tp - 1, rows, columns), bf16),
            pltpu.VMEM((n_tp - 1, rows, columns), bf16),
            dma,
            dma((heads,)),
            dma((back, heads)),
            dma((back, heads)),
            dma((heads * group,)),
            dma((heads * group,)),
            dma((n_tp - 1, tiles)),
            dma((n_tp - 1, tiles)),
        ],
        compiler_params=pltpu.CompilerParams(
            collective_id=0, has_side_effects=True, vmem_limit_bytes=40 << 20
        ),
    )(
        lengths,
        queries.reshape(rows, heads * width),
        pairs.reshape(rows, heads * 2 * head_dim),
        out_proj.reshape(heads * width, model),
    )
    return result.reshape(1, rows, columns)


def solution(mesh):
    sizes = [mesh.shape[axis] for axis in ("segment", "ctx", "tp")]
    return jax.shard_map(
        functools.partial(local, *sizes),
        mesh=mesh,
        in_specs=(
            P("segment", "ctx", "tp", None),
            P("segment", "ctx", "tp", None),
            P("segment", "tp", None, None),
            P(),
        ),
        out_specs=P("segment", "ctx", "tp"),
        check_vma=False,
    )
```
